32 devices in a mesh: gy: 8 (over y, x, core), gx: 4 (over z).
Axes of the slice: x: 2, y: 2, z: 4, core: 2. Of those that a mesh axis runs over, the one named last changes fastest.
Arguments:
- prior_estimate: float32 [4, 192, 80, 128], P(None, 'gy', 'gx'), may hold values from 0.5 to 2
- view_data: bfloat16 [6, 4, 192, 80, 128], P(None, None, 'gy', 'gx'), may hold values from 0.19921875 to 5
- blur_taps: float32 [6, 3, 31], replicated, may hold values from 0.05 to 1
- view_shifts: int32 [6, 2], replicated, may hold values from -2 to 2
- view_extents: int32 [6, 4], replicated, may hold values from 0 to 192, as said below
Outputs:
- estimate: float32 [4, 192, 80, 128], P(None, 'gy', 'gx')
- misfit: float32 [1, 6, 4], replicated
The draws below stay inside these ranges and needn't reach their ends.
Inputs may be any that keep to these rules, and one draw needn't show every extreme that they name: `view_extents`: each row holds first row < end row <= 192 and first column < end column <= 80; view 0 covers the whole volume.
All inputs are finite; a program needn't handle non-finite values.
Results may differ from the reference program's by a relative error of at most 0.0011.
Values may be sent and summed in bfloat16 or wider, within the bound.
No kernel may reach another device: no remote copies, remote signals or barrier semaphores. Data moves between devices by JAX's collectives and lax.ppermute only.
A program may use at most 128 MiB of HBM per device.

```python
import math
import jax
import jax.numpy as jnp
from jax import lax

C = 4
V = 6
TAPS = 31
SMAX = 2
ITERS = 1
Z = 128
NY = 192
NX = 80


def draw_view_extents(key, part):
    key_ylow = jax.random.fold_in(key, 11)
    key_yhigh = jax.random.fold_in(key, 12)
    key_xlow = jax.random.fold_in(key, 13)
    key_xhigh = jax.random.fold_in(key, 14)
    y_low = jax.random.randint(key_ylow, (V,), 0, NY // 2)
    y_high = jax.random.randint(key_yhigh, (V,), NY // 2 + 1, NY + 1)
    x_low = jax.random.randint(key_xlow, (V,), 0, NX // 2)
    x_high = jax.random.randint(key_xhigh, (V,), NX // 2 + 1, NX + 1)
    leading = jnp.arange(V) == 0
    y_low = jnp.where(leading, 0, y_low)
    y_high = jnp.where(leading, NY, y_high)
    x_low = jnp.where(leading, 0, x_low)
    x_high = jnp.where(leading, NX, x_high)
    return jnp.stack([y_low, y_high, x_low, x_high], axis=1).astype(jnp.int32)


def cuboid_layer(key, salt, low_half, high_half):
    layer_key = jax.random.fold_in(key, salt)
    key_period = jax.random.fold_in(layer_key, 1)
    key_offset = jax.random.fold_in(layer_key, 2)
    key_table = jax.random.fold_in(layer_key, 3)
    periods = 2 * jax.random.randint(key_period, (3,), low_half, high_half) + 1
    offsets = jax.random.randint(key_offset, (3,), 0, 1 << 20) % periods
    rows = (jnp.arange(NY, dtype=jnp.int32) + offsets[0]) // periods[0]
    cols = (jnp.arange(NX, dtype=jnp.int32) + offsets[1]) // periods[1]
    depth = (jnp.arange(Z, dtype=jnp.int32) + offsets[2]) // periods[2]
    chan = jnp.arange(C, dtype=jnp.int32)
    hashed = (rows[:, None] * 131 + cols[None, :]) % 4099
    hashed = (hashed[:, :, None] * 137 + depth[None, None, :]) % 4099
    hashed = (hashed[None, :, :, :] * 139 + chan[:, None, None, None]) % 4099
    table = jax.random.uniform(key_table, (4099,), jnp.float32, -0.6931472, 0.6931472)
    return jnp.take(table, hashed)


def draw_prior_estimate(key, part):
    fine = cuboid_layer(key, 21, 1, 5)
    coarse = cuboid_layer(key, 22, 5, 12)
    ypos = jnp.arange(NY, dtype=jnp.float32) / (NY - 1.0) * 2.0 - 1.0
    xpos = jnp.arange(NX, dtype=jnp.float32) / (NX - 1.0) * 2.0 - 1.0
    ramp = 0.5 * ypos[:, None] + 0.3 * xpos[None, :]
    noise = jax.random.uniform(jax.random.fold_in(key, 23), (C, NY, NX, Z), jnp.float32, -0.15, 0.15)
    logged = 0.6 * fine + 0.6 * coarse + ramp[None, :, :, None] + noise
    return jnp.clip(jnp.exp(logged), 0.5, 2.0).astype(jnp.float32)


def place_ends(entries, own_key, smallest, top_value):
    longest = entries.shape.index(max(entries.shape))
    spots = []
    for shift in (0, 1):
        where = [jax.random.randint(jax.random.fold_in(own_key, axis), (), 0, length) for axis, length in enumerate(entries.shape)]
        where[longest] = (where[longest] + shift) % entries.shape[longest]
        spots.append(tuple(where))
    return entries.at[spots[0]].set(smallest).at[spots[1]].set(top_value)


def block_scale(stream_key, dims, cuts, least, top_value):
    gain = 1.0
    for position, parts in cuts:
        steps = jax.random.uniform(jax.random.fold_in(jax.random.fold_in(stream_key, 6), position), (parts,), jnp.float32, least / len(cuts), top_value / len(cuts))
        gain = gain * jnp.repeat(jnp.exp(steps), dims[position] // parts).reshape((-1,) + (1,) * (len(dims) - 1 - position))
    return gain


def setup_inputs(seed: int = 0) -> dict:
    splits = jax.random.split(jax.random.key(seed), 6)
    return {
        "prior_estimate": draw_prior_estimate(jax.random.fold_in(splits[5], 71), 0),
        "view_data": jnp.clip(jnp.exp(math.log(5.0) - 3.2227897 * jax.random.uniform(splits[1], (V, C, NY, NX, Z), jnp.float32) ** block_scale(splits[1], (V, C, NY, NX, Z), ((2, 8), (3, 4)), -0.2, 0.2)), 0.19921875, 5.0).astype(jnp.bfloat16),
        "blur_taps": jnp.clip(jnp.exp(jax.random.uniform(splits[2], (V, 3, TAPS), jnp.float32, math.log(0.05), math.log(1.0))), 0.05, 1.0),
        "view_shifts": place_ends(jax.random.randint(splits[3], (V, 2), 0 - SMAX, SMAX + 1), jax.random.fold_in(splits[3], 1), 0 - SMAX, SMAX).astype(jnp.int32),
        "view_extents": draw_view_extents(jax.random.fold_in(splits[5], 71), 0),
    }


def normalized(blur_taps):
    scaled = blur_taps / jnp.sum(blur_taps, axis=-1, keepdims=True)
    return scaled.astype(jnp.bfloat16).astype(jnp.float32)


def correlate(field, kernel, axis_pos, offset):
    tap_count = kernel.shape[0]
    half_span = (tap_count - 1) // 2
    reach_span = half_span + SMAX
    widths = [(0, 0)] * field.ndim
    widths[axis_pos] = (reach_span, reach_span)
    padded = jnp.pad(field.astype(jnp.float32), widths)
    extent = field.shape[axis_pos]
    start_at = (offset + SMAX).astype(jnp.int32)
    moved = lax.dynamic_slice_in_dim(padded, start_at, extent + 2 * half_span, axis_pos)
    total = jnp.zeros(field.shape, jnp.float32)
    for tap in range(tap_count):
        total = total + kernel[tap] * lax.slice_in_dim(moved, tap, tap + extent, axis=axis_pos)
    return total


def reference(prior_estimate, view_data, blur_taps, view_shifts, view_extents):
    kernels = normalized(blur_taps)
    flipped = kernels[:, :, ::-1]
    view_count = view_data.shape[0]
    row_ids = jnp.arange(prior_estimate.shape[1], dtype=jnp.int32)
    col_ids = jnp.arange(prior_estimate.shape[2], dtype=jnp.int32)
    zero_shift = jnp.zeros((), jnp.int32)
    estimate = prior_estimate
    misfit_rows = []
    for step in range(ITERS):
        estimate_low = estimate.astype(jnp.bfloat16)
        total = jnp.zeros(estimate.shape, jnp.float32)
        terms = []
        for view in range(view_count):
            shift_y = view_shifts[view, 0]
            shift_x = view_shifts[view, 1]
            rows_in = (row_ids >= view_extents[view, 0]) & (row_ids < view_extents[view, 1])
            cols_in = (col_ids >= view_extents[view, 2]) & (col_ids < view_extents[view, 3])
            covered = (rows_in[:, None] & cols_in[None, :])[None, :, :, None]
            blurred_y = correlate(estimate_low, kernels[view, 0], 1, shift_y).astype(jnp.bfloat16)
            blurred_x = correlate(blurred_y, kernels[view, 1], 2, shift_x).astype(jnp.bfloat16)
            predicted = correlate(blurred_x, kernels[view, 2], 3, zero_shift)
            measured = view_data[view].astype(jnp.float32)
            ratio = jnp.where(covered, measured / predicted, 1.0).astype(jnp.bfloat16)
            diverge = jnp.where(covered, measured * jnp.log(measured / predicted) - measured + predicted, 0.0)
            terms.append(jnp.sum(diverge, axis=(1, 2, 3)))
            back_z = correlate(ratio, flipped[view, 2], 3, zero_shift).astype(jnp.bfloat16)
            back_y = correlate(back_z, flipped[view, 0], 1, -shift_y)
            back_x = correlate(back_y, flipped[view, 1], 2, -shift_x)
            total = total + back_x
        estimate = estimate * (total / view_count)
        misfit_rows.append(jnp.stack(terms))
    return estimate, jnp.stack(misfit_rows)
```

```python
import functools

import jax
import jax.numpy as jnp
from jax import lax
from jax.experimental import pallas as pl
from jax.experimental.pallas import tpu as pltpu
from jax.sharding import PartitionSpec as P

SMAX = 2
GROUP = 16


def normalized(blur_taps):
    scaled = blur_taps / jnp.sum(blur_taps, axis=-1, keepdims=True)
    return scaled.astype(jnp.bfloat16).astype(jnp.float32)


def banded(taps, lag):
    view_count, tap_count = taps.shape
    rest = (1,) * (lag.ndim - 1)
    total = jnp.zeros(lag.shape, jnp.float32)
    for tap in range(tap_count):
        total = jnp.where(lag == tap, taps[:, tap].reshape((view_count,) + rest), total)
    return total


def iota(shape, dim):
    return lax.broadcasted_iota(jnp.int32, shape, dim)


def kron_rows(table, group):
    view_count, rows, cols = table.shape
    spread = (iota((cols, cols * group), 0) == iota((cols, cols * group), 1) // group).astype(
        jnp.bfloat16
    )
    wide = jnp.einsum(
        "vab,bc->vac", table.astype(jnp.bfloat16), spread, preferred_element_type=jnp.float32
    )
    diag = iota((group, cols * group), 0) == iota((group, cols * group), 1) % group
    full = jnp.where(diag[None, None], wide[:, :, None, :], 0.0).astype(jnp.bfloat16)
    return full.reshape(view_count, rows * group, cols * group)


def fused_kernel(
    dims,
    where_ref,
    frame_ref,
    data_ref,
    ty_ref,
    tyt_ref,
    kx_ref,
    kxt_ref,
    tz_ref,
    tzt_ref,
    low_ref,
    mid_ref,
    high_ref,
    misfit_ref,
    mixed_ref,
):
    view_count, height, breadth, reach = dims
    wide, _, lanes = frame_ref.shape
    rows = 2 * height
    per_view = rows // GROUP

    def blur_y(x, carry):
        mixed_ref[x] = jnp.dot(
            ty_ref[...], frame_ref[x], preferred_element_type=jnp.float32
        ).astype(jnp.bfloat16)
        return carry

    lax.fori_loop(0, wide, blur_y, 0, unroll=2)

    odd = where_ref[view_count * 4]
    chip_row = where_ref[view_count * 4 + 1]
    first_col = where_ref[view_count * 4 + 2]
    misfit_ref[...] = jnp.zeros_like(misfit_ref)

    def one_group(step, carry):
        view = step // per_view
        part = step % per_view
        spot = pl.ds(pl.multiple_of(step * GROUP, GROUP), GROUP)
        place = pl.ds(pl.multiple_of(part * GROUP, GROUP), GROUP)
        block = mixed_ref[:, spot, :].reshape(wide * GROUP, lanes)
        blurred_x = jnp.dot(kx_ref[view], block, preferred_element_type=jnp.float32).astype(
            jnp.bfloat16
        )
        predicted = jnp.dot(blurred_x, tz_ref[view], preferred_element_type=jnp.float32)
        predicted = predicted.reshape(breadth, GROUP, lanes)
        measured = data_ref[view, :, place, :].astype(jnp.float32)
        order = part * GROUP + lax.broadcasted_iota(jnp.int32, predicted.shape, 1)
        swapped = jnp.where(order < height, order + height, order - height)
        row = chip_row + jnp.where(odd == 1, swapped, order)
        col = first_col + lax.broadcasted_iota(jnp.int32, predicted.shape, 0)
        covered = (row >= where_ref[view * 4]) & (row < where_ref[view * 4 + 1])
        covered &= (col >= where_ref[view * 4 + 2]) & (col < where_ref[view * 4 + 3])
        quotient = measured / predicted
        diverge = jnp.where(covered, measured * jnp.log(quotient) - measured + predicted, 0.0)
        misfit_ref[view] += jnp.sum(diverge, axis=0)
        ratio = jnp.where(covered, quotient, 1.0).astype(jnp.bfloat16)
        back_z = jnp.dot(
            ratio.reshape(breadth * GROUP, lanes), tzt_ref[view], preferred_element_type=jnp.float32
        ).astype(jnp.bfloat16)
        spread = jnp.dot(kxt_ref[view], back_z, preferred_element_type=jnp.float32)
        mixed_ref[:, spot, :] = spread.astype(jnp.bfloat16).reshape(wide, GROUP, lanes)
        return carry

    lax.fori_loop(0, view_count * per_view, one_group, 0)

    def spread_y(x):
        return jnp.dot(tyt_ref[...], mixed_ref[x], preferred_element_type=jnp.float32)

    def edge(x, carry):
        low_ref[x] = spread_y(x).astype(jnp.bfloat16)
        high_ref[x] = spread_y(reach + breadth + x).astype(jnp.bfloat16)
        return carry

    lax.fori_loop(0, reach, edge, 0)

    def middle(x, carry):
        mid_ref[x] = spread_y(reach + x)
        return carry

    lax.fori_loop(0, breadth, middle, 0, unroll=2)


def per_device(prior_estimate, view_data, blur_taps, view_shifts, view_extents):
    channels, height, breadth, length = prior_estimate.shape
    view_count = view_data.shape[0]
    half_span = (blur_taps.shape[-1] - 1) // 2
    reach = half_span + SMAX
    half = channels // 2
    lanes = half * length
    wide = breadth + 2 * reach
    gy_count = lax.axis_size("gy")
    gx_count = lax.axis_size("gx")
    gy = lax.axis_index("gy")
    odd = gy % 2

    swap = [(i, i ^ 1) for i in range(gy_count)]
    near = [(i, i + 1) for i in range(1, gy_count - 1, 2)]
    near += [(target, source) for source, target in near]
    far = [(i, i + 2) for i in range(1, gy_count - 2, 2)] + [
        (i, i - 2) for i in range(2, gy_count, 2)
    ]
    far_back = [(target, source) for source, target in far]
    up = [(i, i + 1) for i in range(gx_count - 1)]
    down = [(target, source) for source, target in up]

    halves = prior_estimate.astype(jnp.bfloat16).reshape(2, half, height, breadth, length)
    halves = halves.transpose(0, 3, 2, 1, 4).reshape(2, breadth, height, lanes)
    keep = lax.dynamic_index_in_dim(halves, odd, 0, keepdims=False)
    other = lax.dynamic_index_in_dim(halves, 1 - odd, 0, keepdims=False)
    tall = jnp.concatenate(
        [
            lax.ppermute(other, "gy", near),
            keep,
            lax.ppermute(other, "gy", swap),
            lax.ppermute(keep, "gy", far),
        ],
        axis=1,
    )
    frame = jnp.concatenate(
        [
            lax.ppermute(tall[breadth - reach :], "gx", up),
            tall,
            lax.ppermute(tall[:reach], "gx", down),
        ],
        axis=0,
    )

    data_keep = lax.dynamic_slice_in_dim(view_data, half * odd, half, axis=1)
    data_other = lax.dynamic_slice_in_dim(view_data, half * (1 - odd), half, axis=1)
    data = jnp.concatenate([data_keep, lax.ppermute(data_other, "gy", swap)], axis=2)
    data = data.transpose(0, 3, 2, 1, 4).reshape(view_count, breadth, 2 * height, lanes)

    kernels = normalized(blur_taps)
    shift_y = view_shifts[:, 0][:, None, None]
    shift_x = view_shifts[:, 1][:, None, None]
    spot = iota((view_count, 2 * height, 4 * height), 2)
    block = spot // height
    source_row = jnp.where(odd == 0, block - 1, 2 - block) * height + spot % height
    spot = iota((view_count, 2 * height, 4 * height), 1) + height
    block = spot // height
    target_row = jnp.where(odd == 0, block - 1, 2 - block) * height + spot % height
    table_y = banded(kernels[:, 0], source_row - target_row - shift_y + half_span)
    table_y = table_y.astype(jnp.bfloat16).reshape(view_count * 2 * height, 4 * height)
    source_col = iota((view_count, breadth, wide), 2) - reach
    lag_x = source_col - iota((view_count, breadth, wide), 1) - shift_x + half_span
    table_x = banded(kernels[:, 1], lag_x)
    lag_z = iota((view_count, length, length), 1) - iota((view_count, length, length), 2)
    eye = jnp.eye(half, dtype=jnp.float32)

    def paired(table):
        table = eye[None, :, None, :, None] * table[:, None, :, None, :]
        return table.reshape(view_count, lanes, lanes).astype(jnp.bfloat16)

    table_z = paired(banded(kernels[:, 2], lag_z + half_span))
    table_zt = paired(banded(kernels[:, 2], half_span - lag_z))
    kron_x = kron_rows(table_x, GROUP)
    kron_xt = kron_rows(table_x.transpose(0, 2, 1), GROUP)
    places = jnp.concatenate(
        [
            view_extents.reshape(-1),
            jnp.stack([odd, (gy - odd) * height, lax.axis_index("gx") * breadth]),
        ]
    ).astype(jnp.int32)

    vmem = pl.BlockSpec(memory_space=pltpu.VMEM)
    low, mid, high, sums = pl.pallas_call(
        functools.partial(fused_kernel, (view_count, height, breadth, reach)),
        in_specs=[pl.BlockSpec(memory_space=pltpu.SMEM)] + [vmem] * 8,
        out_specs=[vmem] * 4,
        out_shape=[
            jax.ShapeDtypeStruct((reach, 4 * height, lanes), jnp.bfloat16),
            jax.ShapeDtypeStruct((breadth, 4 * height, lanes), jnp.float32),
            jax.ShapeDtypeStruct((reach, 4 * height, lanes), jnp.bfloat16),
            jax.ShapeDtypeStruct((view_count, GROUP, lanes), jnp.float32),
        ],
        scratch_shapes=[pltpu.VMEM((wide, view_count * 2 * height, lanes), jnp.bfloat16)],
        compiler_params=pltpu.CompilerParams(vmem_limit_bytes=56 << 20),
        name="blur_and_back",
    )(places, frame, data, table_y, table_y.T, kron_x, kron_xt, table_z, table_zt)

    from_left = lax.ppermute(high, "gx", up).astype(jnp.float32)
    from_right = lax.ppermute(low, "gx", down).astype(jnp.float32)
    pad = ((0, breadth - reach), (0, 0), (0, 0))
    mid = mid + jnp.pad(from_left, pad) + jnp.pad(from_right, (pad[0][::-1],) + pad[1:])
    near_part = lax.ppermute(mid[:, :height].astype(jnp.bfloat16), "gy", near)
    swap_part = lax.ppermute(mid[:, 2 * height : 3 * height], "gy", swap)
    far_part = lax.ppermute(mid[:, 3 * height :].astype(jnp.bfloat16), "gy", far_back)
    kept = mid[:, height : 2 * height] + far_part.astype(jnp.float32)
    given = swap_part + near_part.astype(jnp.float32)
    both = jnp.where(
        odd == 0, jnp.stack([kept, given]), jnp.stack([given, kept])
    )
    total = both.reshape(2, breadth, height, half, length).transpose(0, 3, 2, 1, 4)
    total = total.reshape(channels, height, breadth, length)
    estimate = prior_estimate * (total / view_count)

    sums = jnp.sum(sums.reshape(view_count, GROUP, half, length), axis=(1, 3))
    sums = lax.dynamic_update_slice(
        jnp.zeros((view_count, channels), jnp.float32), sums, (jnp.int32(0), half * odd)
    )
    everyone = gy_count * gx_count
    sums = jnp.broadcast_to(sums.reshape(1, -1), (everyone, view_count * channels))
    sums = lax.all_to_all(sums, ("gy", "gx"), 0, 0)
    misfit = jnp.sum(sums, axis=0).reshape(1, view_count, channels)
    return (estimate, misfit)


def solution(mesh):
    in_specs = (P(None, "gy", "gx", None), P(None, None, "gy", "gx", None), P(), P(), P())
    out_specs = (P(None, "gy", "gx", None), P())
    return jax.shard_map(
        per_device, mesh=mesh, in_specs=in_specs, out_specs=out_specs, check_vma=False
    )
```
